32 devices in a mesh: pop: 16 (over z, y, core), out: 2 (over x).
Axes of the slice: x: 2, y: 2, z: 4, core: 2. Of those that a mesh axis runs over, the one named last changes fastest.
Arguments:
- inputs: bfloat16 [6144, 4096], P(('pop', 'out')), may hold values from -6 to 6
- projection: bfloat16 [4096, 4096], P('pop', 'out'), may hold values from -0.09375 to 0.09375
- factor_a: bfloat16 [1536, 4096], P(('pop', 'out')), may hold values from -0.09375 to 0.09375
- factor_b: bfloat16 [1536, 4096], P('pop', 'out'), may hold values from -6 to 6
- fitness_w: float32 [1536], P('pop'), may hold values from -5 to 5
- elite_idx: int32 [384], P('pop'), may hold values from 0 to 95, as said below
Outputs:
- outputs: bfloat16 [6144, 4096], P('pop', 'out')
- update: float32 [4096, 4096], P('pop', 'out')
The draws below stay inside these ranges and needn't reach their ends.
Inputs may be any that keep to these rules, and one draw needn't show every extreme that they name: `elite_idx`: the 24 entries of each aligned block of 24 are distinct members of that block's group.
All inputs are finite; a program needn't handle non-finite values.
Results may differ from the reference program's by a relative error of at most 0.0029.
Values may be sent and summed in bfloat16 or wider, within the bound.
A program may use at most 64 MiB of HBM per device.

```python
import math
import jax
import jax.numpy as jnp
from jax import lax

D_IN = 4096
D_OUT = 4096
MEM = 96
TOK_MEM = 4
ELITE = 24
MEMBERS = 1536
ELITES = 384
N_POP = 16


def pick_group(group_key):
    return jax.random.permutation(group_key, MEM)[:ELITE]


def draw_elite_idx(key, part):
    group_keys = jax.random.split(key, ELITES // ELITE)
    picks = jax.vmap(pick_group)(group_keys)
    return picks.reshape(-1).astype(jnp.int32)


def block_levels(own_key, extent, shards, least, top_value):
    gain, own = 1.0, jax.random.fold_in(own_key, 6)
    for dim, shards_of in shards:
        heights = jnp.exp(jax.random.uniform(jax.random.fold_in(own, dim), (shards_of,), jnp.float32, least / len(shards), top_value / len(shards)))
        gain = gain * jnp.repeat(heights, extent[dim] // shards_of).reshape([-1 if axis == dim else 1 for axis in range(len(extent))])
    return gain


def noise(rng, shape, width, most, cuts=(), kind=jnp.bfloat16):
    drawn = width * jax.random.normal(rng, shape, jnp.float32)
    if cuts:
        drawn = drawn * block_levels(rng, shape, cuts, -0.22, 0.18)
    return jnp.clip(drawn, -most, most).astype(kind)


def setup_inputs(seed: int = 0) -> dict:
    key_of = jax.random.split(jax.random.key(seed), 7)
    inputs = noise(key_of[0], (MEMBERS * TOK_MEM, D_IN), 1.0, 6.0, ((0, 32),))
    projection = noise(key_of[1], (D_IN, D_OUT), D_IN ** -0.5, 0.09375, ((0, 16), (1, 2)))
    factor_a = noise(key_of[2], (MEMBERS, D_IN), D_IN ** -0.5, 0.09375, ((0, 32),))
    factor_b = noise(key_of[3], (MEMBERS, D_OUT), 1.0, 6.0, ((0, 16), (1, 2)))
    fitness_w = noise(key_of[4], (MEMBERS,), 1.0, 5.0, ((0, 16),), jnp.float32)
    elite_idx = draw_elite_idx(jax.random.fold_in(key_of[6], 71), 0)
    return {"inputs": inputs, "projection": projection, "factor_a": factor_a, "factor_b": factor_b, "fitness_w": fitness_w, "elite_idx": elite_idx}


def reference(inputs, projection, factor_a, factor_b, fitness_w, elite_idx):
    grouped_rows = inputs.reshape(N_POP, MEM, TOK_MEM, D_IN)
    grouped_a = factor_a.reshape(N_POP, MEM, D_IN)

    def group_dot(pair):
        rows_here, factors_here = pair
        return jnp.einsum('mtd,md->mt', rows_here.astype(jnp.float32), factors_here.astype(jnp.float32))
    member_dot = lax.map(group_dot, (grouped_rows, grouped_a)).reshape(-1)
    projected = jnp.dot(inputs, projection, preferred_element_type=jnp.float32)
    spread_factor = jnp.repeat(factor_b.astype(jnp.float32), TOK_MEM, axis=0)
    outputs = (projected + member_dot[:, None] * spread_factor).astype(jnp.bfloat16)
    chosen = jnp.arange(ELITES, dtype=jnp.int32) // ELITE * MEM + elite_idx.astype(jnp.int32)
    scaled = (fitness_w[chosen][:, None] * factor_a[chosen].astype(jnp.float32)).astype(jnp.bfloat16)
    update = jnp.dot(scaled.T, factor_b[chosen], preferred_element_type=jnp.float32) * math.sqrt(D_IN / ELITES)
    return (outputs, update)
```

```python
import functools
import math

import jax
import jax.numpy as jnp
from jax import lax
from jax.experimental import pallas as pl
from jax.experimental.pallas import tpu as pltpu
from jax.sharding import PartitionSpec as P

MESH = pl.DeviceIdType.MESH
F32, BF16 = jnp.float32, jnp.bfloat16
CORES, Y = 2, 2


def chip_at(pos, n_chip):
    z_len = n_chip // Y
    y = pos // z_len
    z = pos * (1 - y) + (n_chip - 1 - pos) * y
    return z * Y + y


def kernel(
    n_pop, n_out, pieces, scale,
    x_ref, w_ref, a_ref, b_ref, f_ref, e_ref,
    out_ref, upd_ref,
    wbuf, bbuf, x_all, a_all, s_src, s_all, acc,
    ring_send, ring_recv, pair_send, pair_recv,
    xs_send, xs_recv, as_send, as_recv, s_send, s_recv, loc_sem,
):
    n_chip = n_pop // CORES
    z_len = n_chip // Y
    p, o = lax.axis_index("pop"), lax.axis_index("out")
    core, chip = p % CORES, p // CORES
    y, z = chip % Y, chip // Y
    pos = z * (1 - y) + (n_chip - 1 - z) * y
    kd, n_cols = w_ref.shape
    nh = n_cols // 2
    rows, d_in = x_ref.shape
    members = a_ref.shape[0]
    per_member = rows // members
    elite = e_ref.shape[0]
    depth = kd // pieces

    nxt = chip_at((pos + 1) % n_chip, n_chip) * CORES + core
    prv = chip_at((pos + n_chip - 1) % n_chip, n_chip) * CORES + core
    to = (nxt, prv)
    pair = chip * CORES + (1 - core)

    x_own = pltpu.make_async_copy(x_ref, x_all.at[o], loc_sem.at[0])
    a_own = pltpu.make_async_copy(a_ref, a_all.at[o], loc_sem.at[1])
    w_own = [
        pltpu.make_async_copy(
            w_ref.at[:, pl.ds(d * nh, nh)],
            wbuf.at[d, 0, pl.ds(pl.multiple_of(core * kd, kd), kd)],
            loc_sem.at[2 + d],
        )
        for d in range(2)
    ]
    for own in (a_own, x_own, *w_own):
        own.start()

    barrier = pltpu.get_barrier_semaphore()
    for k in range(1, n_pop):
        pl.semaphore_signal(
            barrier, inc=1, device_id={"pop": (p + k) % n_pop}, device_id_type=MESH
        )
    for k in range(1, n_out):
        pl.semaphore_signal(
            barrier, inc=1, device_id={"out": (o + k) % n_out}, device_id_type=MESH
        )
    pl.semaphore_wait(barrier, n_pop - 1 + n_out - 1)

    def piece(d, t, s, c):
        if s == pieces:
            return bbuf.at[d, t, c]
        return wbuf.at[
            d, t, pl.ds(pl.multiple_of(c * kd + s * depth, depth), depth)
        ]

    def source(d, t, s):
        if t == 0 and s < pieces:
            return w_ref.at[pl.ds(s * depth, depth), pl.ds(d * nh, nh)]
        return piece(d, t, s, core)

    def ring(d, t, s):
        return pltpu.make_async_remote_copy(
            src_ref=source(d, t, s),
            dst_ref=piece(d, t + 1, s, core),
            send_sem=ring_send.at[d, t, s],
            recv_sem=ring_recv.at[d, t, s],
            device_id={"pop": to[d]},
            device_id_type=MESH,
        )

    def across(d, t, s, c):
        return pltpu.make_async_remote_copy(
            src_ref=source(d, t, s) if c is core else piece(d, t, s, c),
            dst_ref=piece(d, t, s, c),
            send_sem=pair_send.at[d, t, s],
            recv_sem=pair_recv.at[d, t, s],
            device_id={"pop": pair},
            device_id_type=MESH,
        )

    def shared(k, src, dst, send, recv):
        return pltpu.make_async_remote_copy(
            src_ref=src,
            dst_ref=dst,
            send_sem=send.at[k],
            recv_sem=recv.at[k],
            device_id={"out": (o + k) % n_out},
            device_id_type=MESH,
        )

    def block_to(k):
        return pltpu.make_async_remote_copy(
            src_ref=s_src.at[(p + k) % n_pop],
            dst_ref=s_all.at[p],
            send_sem=s_send.at[k],
            recv_sem=s_recv.at[k],
            device_id={"pop": (p + k) % n_pop},
            device_id_type=MESH,
        )

    order = [0, pieces, *range(1, pieces)]
    for s in range(pieces):
        for d in range(2):
            ring(d, 0, s).start()
            across(d, 0, s, core).start()
        if s == 0:
            for k in range(1, n_out):
                shared(k, a_ref, a_all.at[o], as_send, as_recv).start()
            for k in range(1, n_out):
                shared(k, x_ref, x_all.at[o], xs_send, xs_recv).start()
            ids = e_ref[...]

            def picks(m):
                at = lax.broadcasted_iota(jnp.int32, (elite, members), 1) + m * members
                return (at == ids).astype(F32).astype(BF16)

            for d in range(2):
                total = jnp.zeros((elite, nh), F32)
                for m in range(n_out):
                    total += jnp.dot(
                        picks(m), b_ref[m, :, d * nh : (d + 1) * nh],
                        preferred_element_type=F32,
                    )
                bbuf[d, 0, core] = total.astype(BF16)
            upd_ref[...] = jnp.zeros_like(upd_ref)
    for d in range(2):
        ring(d, 0, pieces).start()
        across(d, 0, pieces, core).start()

    a_own.wait()
    for k in range(1, n_out):
        shared(k, a_ref, a_all.at[o], as_send, as_recv).wait_recv()
    every = lax.broadcasted_iota(jnp.int32, (elite, n_out * members), 1)
    weight = jnp.sum(jnp.where(every == ids, f_ref[...], 0.0), axis=1, keepdims=True)
    for q in range(n_pop):
        block = jnp.zeros((elite, kd), F32)
        for m in range(n_out):
            block += jnp.dot(
                picks(m), a_all[m, :, q * kd : (q + 1) * kd],
                preferred_element_type=F32,
            )
        s_src[q] = (weight * block).astype(BF16)
    s_all[p] = s_src[p]
    for k in range(1, n_pop):
        block_to(k).start()

    for own in w_own:
        own.wait()

    def chip_of(d, t):
        return chip_at((pos + (n_chip - t if d == 0 else t)) % n_chip, n_chip)

    tile = min(nh, 512)

    def project(d, t):
        off = pl.multiple_of(chip_of(d, t) * (CORES * kd), CORES * kd)
        x_part = x_all[:, :, pl.ds(off, CORES * kd)].reshape(n_out * rows, CORES * kd)
        for j in range(nh // tile):
            lo = d * nh + j * tile
            acc[:, lo : lo + tile] += jnp.dot(
                x_part, wbuf[d, t, :, j * tile : (j + 1) * tile],
                preferred_element_type=F32,
            )

    def update(d, t):
        for c in range(CORES):
            upd_ref[:, d * nh : (d + 1) * nh] += lax.dot_general(
                s_all[chip_of(d, t) * CORES + c], bbuf[d, t, c],
                (((0,), (0,)), ((), ())), preferred_element_type=F32,
            )

    def start_rows():
        x_own.wait()
        for k in range(1, n_out):
            shared(k, x_ref, x_all.at[o], xs_send, xs_recv).wait_recv()
        row = lax.broadcasted_iota(jnp.int32, (rows, members), 0) // per_member
        own = row == lax.broadcasted_iota(jnp.int32, (rows, members), 1)
        for m in range(n_out):
            dots = lax.dot_general(
                x_all[m], a_all[m], (((1,), (1,)), ((), ())),
                preferred_element_type=F32,
            )
            dots = jnp.where(own, dots, 0.0)
            high = dots.astype(BF16)
            rest = dots - high.astype(F32)
            mid = rest.astype(BF16)
            low = (rest - mid.astype(F32)).astype(BF16)
            for d in range(2):
                cols = slice(d * nh, (d + 1) * nh)
                b_part = b_ref[m, :, cols]
                acc[m * rows : (m + 1) * rows, cols] = (
                    jnp.dot(high, b_part, preferred_element_type=F32)
                    + jnp.dot(mid, b_part, preferred_element_type=F32)
                    + jnp.dot(low, b_part, preferred_element_type=F32)
                )

    def start_update():
        for k in range(1, n_pop):
            block_to(k).wait_recv()

    todo = []
    ready = max(1, n_chip // 2)
    for t in range(n_chip):
        if t == ready:
            todo = [start_rows, start_update] + todo
        for s in order:
            for d in range(2):
                if t:
                    ring(d, t - 1, s).wait_recv()
                    if t < n_chip - 1:
                        ring(d, t, s).start()
                    across(d, t, s, core).start()
            if t >= ready and t < n_chip - 1:
                for _ in range(min(3, len(todo))):
                    todo.pop(0)()
        for s in order:
            for d in range(2):
                across(d, t, s, 1 - core).wait_recv()
        for d in range(2):
            todo.append(functools.partial(update, d, t))
            todo.append(functools.partial(project, d, t))
    for job in todo:
        job()

    upd_ref[...] = upd_ref[...] * scale
    out_ref[...] = acc[...].astype(BF16)

    for t in range(n_chip):
        for s in order:
            for d in range(2):
                if t < n_chip - 1:
                    ring(d, t, s).wait_send()
                across(d, t, s, core).wait_send()
    for k in range(1, n_out):
        shared(k, a_ref, a_all.at[o], as_send, as_recv).wait_send()
        shared(k, x_ref, x_all.at[o], xs_send, xs_recv).wait_send()
    for k in range(1, n_pop):
        block_to(k).wait_send()


def solution(mesh):
    n_pop, n_out = mesh.shape["pop"], mesh.shape["out"]
    n_chip = n_pop // CORES

    def step(inputs, projection, factor_a, factor_b, fitness_w, elite_idx):
        rows, d_in = inputs.shape
        kd, n_cols = projection.shape
        members, elite = factor_a.shape[0], elite_idx.shape[0]
        nh = n_cols // 2
        pieces = min(4, kd // 16)
        scale = math.sqrt(d_in / (n_pop * elite))
        dma = pltpu.SemaphoreType.DMA
        hbm, vmem = pl.BlockSpec(memory_space=pl.ANY), pl.BlockSpec(memory_space=pltpu.VMEM)
        return pl.pallas_call(
            functools.partial(kernel, n_pop, n_out, pieces, scale),
            out_shape=(
                jax.ShapeDtypeStruct((n_out * rows, n_cols), BF16),
                jax.ShapeDtypeStruct((kd, n_cols), F32),
            ),
            in_specs=[hbm, hbm, hbm, vmem, vmem, vmem],
            out_specs=(vmem, vmem),
            scratch_shapes=[
                pltpu.VMEM((2, n_chip, CORES * kd, nh), BF16),
                pltpu.VMEM((2, n_chip, CORES, elite, nh), BF16),
                pltpu.VMEM((n_out, rows, d_in), BF16),
                pltpu.VMEM((n_out, members, d_in), BF16),
                pltpu.VMEM((n_pop, elite, kd), BF16),
                pltpu.VMEM((n_pop, elite, kd), BF16),
                pltpu.VMEM((n_out * rows, n_cols), F32),
                dma((2, n_chip, pieces + 1)),
                dma((2, n_chip, pieces + 1)),
                dma((2, n_chip, pieces + 1)),
                dma((2, n_chip, pieces + 1)),
                dma((n_out,)),
                dma((n_out,)),
                dma((n_out,)),
                dma((n_out,)),
                dma((n_pop,)),
                dma((n_pop,)),
                dma((4,)),
            ],
            compiler_params=pltpu.CompilerParams(
                collective_id=0, has_side_effects=True, vmem_limit_bytes=60 * 2**20
            ),
        )(
            inputs,
            projection,
            factor_a,
            factor_b.reshape(n_out, members, n_cols),
            fitness_w.reshape(1, -1),
            elite_idx.reshape(-1, 1),
        )

    return jax.shard_map(
        step,
        mesh=mesh,
        in_specs=(
            P(("pop", "out"), None),
            P("pop", "out"),
            P(("pop", "out"), None),
            P("pop", "out"),
            P("pop"),
            P("pop"),
        ),
        out_specs=(P("pop", "out"), P("pop", "out")),
        check_vma=False,
    )
```

```python
import functools
import math

import jax
import jax.numpy as jnp
from jax import lax
from jax.experimental import pallas as pl
from jax.experimental.pallas import tpu as pltpu
from jax.sharding import PartitionSpec as P

MESH = pl.DeviceIdType.MESH
F32, BF16 = jnp.float32, jnp.bfloat16
CORES, Y = 2, 2


def chip_at(pos, n_chip):
    z_len = n_chip // Y
    y = pos // z_len
    z = pos * (1 - y) + (n_chip - 1 - pos) * y
    return z * Y + y


def kernel(
    n_pop, n_out, pieces,
    x_ref, w_ref, a_ref, b_hbm, f_hbm, e_hbm,
    acc, upd_ref,
    wbuf, bbuf, x_all, a_all, s_src, s_all, b_ref, f_ref, e_ref,
    ring_send, ring_recv, pair_send, pair_recv,
    xs_send, xs_recv, as_send, as_recv, s_send, s_recv, loc_sem,
):
    n_chip = n_pop // CORES
    z_len = n_chip // Y
    p, o = lax.axis_index("pop"), lax.axis_index("out")
    core, chip = p % CORES, p // CORES
    y, z = chip % Y, chip // Y
    pos = z * (1 - y) + (n_chip - 1 - z) * y
    kd, n_cols = w_ref.shape
    nh = n_cols // 2
    rows, d_in = x_ref.shape
    members = a_ref.shape[0]
    per_member = rows // members
    elite = e_ref.shape[1]
    depth = kd // pieces

    nxt = chip_at((pos + 1) % n_chip, n_chip) * CORES + core
    prv = chip_at((pos + n_chip - 1) % n_chip, n_chip) * CORES + core
    to = (nxt, prv)
    pair = chip * CORES + (1 - core)

    x_own = pltpu.make_async_copy(x_ref, x_all.at[o], loc_sem.at[0])
    a_own = pltpu.make_async_copy(a_ref, a_all.at[o], loc_sem.at[1])
    w_own = [
        pltpu.make_async_copy(
            w_ref.at[:, pl.ds(d * nh, nh)],
            wbuf.at[d, 0, pl.ds(pl.multiple_of(core * kd, kd), kd)],
            loc_sem.at[2 + d],
        )
        for d in range(2)
    ]
    small = [
        pltpu.make_async_copy(src, dst, loc_sem.at[4 + k])
        for k, (src, dst) in enumerate(((e_hbm, e_ref), (b_hbm, b_ref), (f_hbm, f_ref)))
    ]
    for own in (*small, a_own, x_own, *w_own):
        own.start()

    barrier = pltpu.get_barrier_semaphore()
    for k in range(1, n_pop):
        pl.semaphore_signal(
            barrier, inc=1, device_id={"pop": (p + k) % n_pop}, device_id_type=MESH
        )
    for k in range(1, n_out):
        pl.semaphore_signal(
            barrier, inc=1, device_id={"out": (o + k) % n_out}, device_id_type=MESH
        )
    pl.semaphore_wait(barrier, n_pop - 1 + n_out - 1)

    def piece(d, t, s, c):
        if s == pieces:
            return bbuf.at[d, t, c]
        return wbuf.at[
            d, t, pl.ds(pl.multiple_of(c * kd + s * depth, depth), depth)
        ]

    def source(d, t, s):
        if t == 0 and s < pieces:
            return w_ref.at[pl.ds(s * depth, depth), pl.ds(d * nh, nh)]
        return piece(d, t, s, core)

    def ring(d, t, s):
        return pltpu.make_async_remote_copy(
            src_ref=source(d, t, s),
            dst_ref=piece(d, t + 1, s, core),
            send_sem=ring_send.at[d, t, s],
            recv_sem=ring_recv.at[d, t, s],
            device_id={"pop": to[d]},
            device_id_type=MESH,
        )

    def across(d, t, s, c):
        return pltpu.make_async_remote_copy(
            src_ref=source(d, t, s) if c is core else piece(d, t, s, c),
            dst_ref=piece(d, t, s, c),
            send_sem=pair_send.at[d, t, s],
            recv_sem=pair_recv.at[d, t, s],
            device_id={"pop": pair},
            device_id_type=MESH,
        )

    def shared(k, src, dst, send, recv):
        return pltpu.make_async_remote_copy(
            src_ref=src,
            dst_ref=dst,
            send_sem=send.at[k],
            recv_sem=recv.at[k],
            device_id={"out": (o + k) % n_out},
            device_id_type=MESH,
        )

    def block_to(k):
        return pltpu.make_async_remote_copy(
            src_ref=s_src.at[(p + k) % n_pop],
            dst_ref=s_all.at[p],
            send_sem=s_send.at[k],
            recv_sem=s_recv.at[k],
            device_id={"pop": (p + k) % n_pop},
            device_id_type=MESH,
        )

    order = [0, pieces, *range(1, pieces)]
    for s in range(pieces):
        for d in range(2):
            ring(d, 0, s).start()
            across(d, 0, s, core).start()
        if s == 0:
            for k in range(1, n_out):
                shared(k, a_ref, a_all.at[o], as_send, as_recv).start()
            for k in range(1, n_out):
                shared(k, x_ref, x_all.at[o], xs_send, xs_recv).start()
            for own in small:
                own.wait()
            turned = lax.broadcasted_iota(jnp.int32, (elite, elite), 0)
            turned = turned == lax.broadcasted_iota(jnp.int32, (elite, elite), 1)
            ids = jnp.sum(
                jnp.where(turned, e_ref[...].astype(F32), 0.0), axis=1, keepdims=True
            ).astype(jnp.int32)

            def picks(m):
                at = lax.broadcasted_iota(jnp.int32, (elite, members), 1) + m * members
                return (at == ids).astype(F32).astype(BF16)

            for d in range(2):
                total = jnp.zeros((elite, nh), F32)
                for m in range(n_out):
                    total += jnp.dot(
                        picks(m), b_ref[m, :, d * nh : (d + 1) * nh],
                        preferred_element_type=F32,
                    )
                bbuf[d, 0, core] = total.astype(BF16)
            upd_ref[...] = jnp.zeros_like(upd_ref)
    for d in range(2):
        ring(d, 0, pieces).start()
        across(d, 0, pieces, core).start()

    a_own.wait()
    for k in range(1, n_out):
        shared(k, a_ref, a_all.at[o], as_send, as_recv).wait_recv()
    every = lax.broadcasted_iota(jnp.int32, (elite, n_out * members), 1)
    weight = jnp.sum(jnp.where(every == ids, f_ref[...], 0.0), axis=1, keepdims=True)
    for q in range(n_pop):
        block = jnp.zeros((elite, kd), F32)
        for m in range(n_out):
            block += jnp.dot(
                picks(m), a_all[m, :, q * kd : (q + 1) * kd],
                preferred_element_type=F32,
            )
        s_src[q] = (weight * block).astype(BF16)
    s_all[p] = s_src[p]
    for k in range(1, n_pop):
        block_to(k).start()

    for own in w_own:
        own.wait()

    def chip_of(d, t):
        return chip_at((pos + (n_chip - t if d == 0 else t)) % n_chip, n_chip)

    tile = min(nh, 512)

    def project(d, t):
        off = pl.multiple_of(chip_of(d, t) * (CORES * kd), CORES * kd)
        x_part = x_all[:, :, pl.ds(off, CORES * kd)].reshape(n_out * rows, CORES * kd)
        for j in range(nh // tile):
            lo = d * nh + j * tile
            acc[:, lo : lo + tile] += jnp.dot(
                x_part, wbuf[d, t, :, j * tile : (j + 1) * tile],
                preferred_element_type=F32,
            )

    def update(d, t):
        for c in range(CORES):
            upd_ref[:, d * nh : (d + 1) * nh] += lax.dot_general(
                s_all[chip_of(d, t) * CORES + c], bbuf[d, t, c],
                (((0,), (0,)), ((), ())), preferred_element_type=F32,
            )

    def start_rows():
        x_own.wait()
        for k in range(1, n_out):
            shared(k, x_ref, x_all.at[o], xs_send, xs_recv).wait_recv()
        row = lax.broadcasted_iota(jnp.int32, (rows, members), 0) // per_member
        own = row == lax.broadcasted_iota(jnp.int32, (rows, members), 1)
        for m in range(n_out):
            dots = lax.dot_general(
                x_all[m], a_all[m], (((1,), (1,)), ((), ())),
                preferred_element_type=F32,
            )
            dots = jnp.where(own, dots, 0.0)
            high = dots.astype(BF16)
            rest = dots - high.astype(F32)
            mid = rest.astype(BF16)
            low = (rest - mid.astype(F32)).astype(BF16)
            for d in range(2):
                cols = slice(d * nh, (d + 1) * nh)
                b_part = b_ref[m, :, cols]
                acc[m * rows : (m + 1) * rows, cols] = (
                    jnp.dot(high, b_part, preferred_element_type=F32)
                    + jnp.dot(mid, b_part, preferred_element_type=F32)
                    + jnp.dot(low, b_part, preferred_element_type=F32)
                )

    def start_update():
        for k in range(1, n_pop):
            block_to(k).wait_recv()

    todo = []
    ready = max(1, n_chip // 2)
    for t in range(n_chip):
        if t == ready:
            todo = [start_rows, start_update] + todo
        for s in order:
            for d in range(2):
                if t:
                    ring(d, t - 1, s).wait_recv()
                    if t < n_chip - 1:
                        ring(d, t, s).start()
                    across(d, t, s, core).start()
            if t >= ready and t < n_chip - 1:
                for _ in range(min(3, len(todo))):
                    todo.pop(0)()
        for s in order:
            for d in range(2):
                across(d, t, s, 1 - core).wait_recv()
        for d in range(2):
            todo.append(functools.partial(update, d, t))
            todo.append(functools.partial(project, d, t))
    for job in todo:
        job()


    for t in range(n_chip):
        for s in order:
            for d in range(2):
                if t < n_chip - 1:
                    ring(d, t, s).wait_send()
                across(d, t, s, core).wait_send()
    for k in range(1, n_out):
        shared(k, a_ref, a_all.at[o], as_send, as_recv).wait_send()
        shared(k, x_ref, x_all.at[o], xs_send, xs_recv).wait_send()
    for k in range(1, n_pop):
        block_to(k).wait_send()


def solution(mesh):
    n_pop, n_out = mesh.shape["pop"], mesh.shape["out"]
    n_chip = n_pop // CORES

    def step(inputs, projection, factor_a, factor_b, fitness_w, elite_idx):
        rows, d_in = inputs.shape
        kd, n_cols = projection.shape
        members, elite = factor_a.shape[0], elite_idx.shape[0]
        nh = n_cols // 2
        pieces = min(4, kd // 16)
        scale = math.sqrt(d_in / (n_pop * elite))
        dma = pltpu.SemaphoreType.DMA
        hbm, vmem = pl.BlockSpec(memory_space=pltpu.HBM), pl.BlockSpec(memory_space=pltpu.VMEM)
        total, update_sum = pl.pallas_call(
            functools.partial(kernel, n_pop, n_out, pieces),
            out_shape=(
                jax.ShapeDtypeStruct((n_out * rows, n_cols), F32),
                jax.ShapeDtypeStruct((kd, n_cols), F32),
            ),
            in_specs=[hbm] * 6,
            out_specs=(vmem, vmem),
            scratch_shapes=[
                pltpu.VMEM((2, n_chip, CORES * kd, nh), BF16),
                pltpu.VMEM((2, n_chip, CORES, elite, nh), BF16),
                pltpu.VMEM((n_out, rows, d_in), BF16),
                pltpu.VMEM((n_out, members, d_in), BF16),
                pltpu.VMEM((n_pop, elite, kd), BF16),
                pltpu.VMEM((n_pop, elite, kd), BF16),
                pltpu.VMEM((n_out, members, n_cols), BF16),
                pltpu.VMEM((1, n_out * members), F32),
                pltpu.VMEM((1, elite), jnp.int32),
                dma((2, n_chip, pieces + 1)),
                dma((2, n_chip, pieces + 1)),
                dma((2, n_chip, pieces + 1)),
                dma((2, n_chip, pieces + 1)),
                dma((n_out,)),
                dma((n_out,)),
                dma((n_out,)),
                dma((n_out,)),
                dma((n_pop,)),
                dma((n_pop,)),
                dma((7,)),
            ],
            compiler_params=pltpu.CompilerParams(
                collective_id=0, has_side_effects=True, vmem_limit_bytes=44 * 2**20
            ),
        )(
            inputs,
            projection,
            factor_a,
            factor_b.reshape(n_out, members, n_cols),
            fitness_w.reshape(1, -1),
            elite_idx.reshape(1, -1),
        )
        return total.astype(BF16), update_sum * scale

    return jax.shard_map(
        step,
        mesh=mesh,
        in_specs=(
            P(("pop", "out"), None),
            P("pop", "out"),
            P(("pop", "out"), None),
            P("pop", "out"),
            P("pop"),
            P("pop"),
        ),
        out_specs=(P("pop", "out"), P("pop", "out")),
        check_vma=False,
    )
```

```python
import functools
import math

import jax
import jax.numpy as jnp
from jax import lax
from jax.experimental import pallas as pl
from jax.experimental.pallas import tpu as pltpu
from jax.sharding import PartitionSpec as P

MESH = pl.DeviceIdType.MESH
F32, BF16 = jnp.float32, jnp.bfloat16
CORES, Y = 2, 2


def chip_at(pos, n_chip):
    z_len = n_chip // Y
    y = pos // z_len
    z = pos * (1 - y) + (n_chip - 1 - pos) * y
    return z * Y + y


def kernel(
    n_pop, n_out, pieces,
    x_ref, w_ref, a_ref, b_hbm, f_hbm, e_hbm,
    acc, upd_ref,
    wbuf, bbuf, x_all, a_all, s_src, s_all, b_ref, f_ref, e_ref,
    ring_send, ring_recv, pair_send, pair_recv,
    xs_send, xs_recv, as_send, as_recv, s_send, s_recv, loc_sem,
):
    n_chip = n_pop // CORES
    z_len = n_chip // Y
    p, o = lax.axis_index("pop"), lax.axis_index("out")
    core, chip = p % CORES, p // CORES
    y, z = chip % Y, chip // Y
    pos = z * (1 - y) + (n_chip - 1 - z) * y
    kd, n_cols = w_ref.shape
    nh = n_cols // 2
    rows, d_in = x_ref.shape
    members = a_ref.shape[0]
    per_member = rows // members
    elite = e_ref.shape[1]
    depth = kd // pieces

    nxt = chip_at((pos + 1) % n_chip, n_chip) * CORES + core
    prv = chip_at((pos + n_chip - 1) % n_chip, n_chip) * CORES + core
    to = (nxt, prv)
    pair = chip * CORES + (1 - core)

    x_own = pltpu.make_async_copy(x_ref, x_all.at[o], loc_sem.at[0])
    a_own = pltpu.make_async_copy(a_ref, a_all.at[o], loc_sem.at[1])
    w_own = [
        pltpu.make_async_copy(
            w_ref.at[:, pl.ds(d * nh, nh)],
            wbuf.at[d, 0, pl.ds(pl.multiple_of(core * kd, kd), kd)],
            loc_sem.at[2 + d],
        )
        for d in range(2)
    ]
    small = [
        pltpu.make_async_copy(src, dst, loc_sem.at[4 + k])
        for k, (src, dst) in enumerate(((e_hbm, e_ref), (b_hbm, b_ref), (f_hbm, f_ref)))
    ]
    for own in (*small, a_own, x_own, *w_own):
        own.start()

    barrier = pltpu.get_barrier_semaphore()
    for k in range(1, n_pop):
        pl.semaphore_signal(
            barrier, inc=1, device_id={"pop": (p + k) % n_pop}, device_id_type=MESH
        )
    for k in range(1, n_out):
        pl.semaphore_signal(
            barrier, inc=1, device_id={"out": (o + k) % n_out}, device_id_type=MESH
        )
    pl.semaphore_wait(barrier, n_pop - 1 + n_out - 1)

    def piece(d, t, s, c):
        if s == pieces:
            return bbuf.at[d, t, c]
        return wbuf.at[
            d, t, pl.ds(pl.multiple_of(c * kd + s * depth, depth), depth)
        ]

    def source(d, t, s):
        if t == 0 and s < pieces:
            return w_ref.at[pl.ds(s * depth, depth), pl.ds(d * nh, nh)]
        return piece(d, t, s, core)

    def ring(d, t, s):
        return pltpu.make_async_remote_copy(
            src_ref=source(d, t, s),
            dst_ref=piece(d, t + 1, s, core),
            send_sem=ring_send.at[d, t, s],
            recv_sem=ring_recv.at[d, t, s],
            device_id={"pop": to[d]},
            device_id_type=MESH,
        )

    def across(d, t, s, c):
        return pltpu.make_async_remote_copy(
            src_ref=source(d, t, s) if c is core else piece(d, t, s, c),
            dst_ref=piece(d, t, s, c),
            send_sem=pair_send.at[d, t, s],
            recv_sem=pair_recv.at[d, t, s],
            device_id={"pop": pair},
            device_id_type=MESH,
        )

    def shared(k, src, dst, send, recv):
        return pltpu.make_async_remote_copy(
            src_ref=src,
            dst_ref=dst,
            send_sem=send.at[k],
            recv_sem=recv.at[k],
            device_id={"out": (o + k) % n_out},
            device_id_type=MESH,
        )

    def block_to(k):
        return pltpu.make_async_remote_copy(
            src_ref=s_src.at[(p + k) % n_pop],
            dst_ref=s_all.at[p],
            send_sem=s_send.at[k],
            recv_sem=s_recv.at[k],
            device_id={"pop": (p + k) % n_pop},
            device_id_type=MESH,
        )

    order = [0, pieces, *range(1, pieces)]
    for s in range(pieces):
        for d in range(2):
            ring(d, 0, s).start()
            across(d, 0, s, core).start()
        if s == 0:
            for k in range(1, n_out):
                shared(k, a_ref, a_all.at[o], as_send, as_recv).start()
            for k in range(1, n_out):
                shared(k, x_ref, x_all.at[o], xs_send, xs_recv).start()
            for own in small:
                own.wait()
            turned = lax.broadcasted_iota(jnp.int32, (elite, elite), 0)
            turned = turned == lax.broadcasted_iota(jnp.int32, (elite, elite), 1)
            ids = jnp.sum(
                jnp.where(turned, e_ref[...].astype(F32), 0.0), axis=1, keepdims=True
            ).astype(jnp.int32)

            def picks(m):
                at = lax.broadcasted_iota(jnp.int32, (elite, members), 1) + m * members
                return (at == ids).astype(F32).astype(BF16)

            for d in range(2):
                total = jnp.zeros((elite, nh), F32)
                for m in range(n_out):
                    total += jnp.dot(
                        picks(m), b_ref[m, :, d * nh : (d + 1) * nh],
                        preferred_element_type=F32,
                    )
                bbuf[d, 0, core] = total.astype(BF16)
            upd_ref[...] = jnp.zeros_like(upd_ref)
    for d in range(2):
        ring(d, 0, pieces).start()
        across(d, 0, pieces, core).start()

    a_own.wait()
    for k in range(1, n_out):
        shared(k, a_ref, a_all.at[o], as_send, as_recv).wait_recv()
    every = lax.broadcasted_iota(jnp.int32, (elite, n_out * members), 1)
    weight = jnp.sum(jnp.where(every == ids, f_ref[...], 0.0), axis=1, keepdims=True)
    for q in range(n_pop):
        block = jnp.zeros((elite, kd), F32)
        for m in range(n_out):
            block += jnp.dot(
                picks(m), a_all[m, :, q * kd : (q + 1) * kd],
                preferred_element_type=F32,
            )
        s_src[q] = (weight * block).astype(BF16)
    s_all[p] = s_src[p]
    for k in range(1, n_pop):
        block_to(k).start()

    for own in w_own:
        own.wait()

    def chip_of(d, t):
        return chip_at((pos + (n_chip - t if d == 0 else t)) % n_chip, n_chip)

    tile = min(nh, 512)

    def project(d, t, parts=1, part=0):
        off = pl.multiple_of(chip_of(d, t) * (CORES * kd), CORES * kd)
        x_part = x_all[:, :, pl.ds(off, CORES * kd)].reshape(n_out * rows, CORES * kd)
        take = kd // parts
        for j in range(nh // tile):
            lo, cols = d * nh + j * tile, slice(j * tile, (j + 1) * tile)
            if parts == 1:
                more = jnp.dot(x_part, wbuf[d, t, :, cols], preferred_element_type=F32)
            else:
                more = 0.0
                for c in range(CORES):
                    at = c * kd + part * take
                    more += jnp.dot(
                        x_part[:, at : at + take], wbuf[d, t, at : at + take, cols],
                        preferred_element_type=F32,
                    )
            acc[:, lo : lo + tile] += more

    def update(d, t):
        for c in range(CORES):
            upd_ref[:, d * nh : (d + 1) * nh] += lax.dot_general(
                s_all[chip_of(d, t) * CORES + c], bbuf[d, t, c],
                (((0,), (0,)), ((), ())), preferred_element_type=F32,
            )

    def start_rows():
        x_own.wait()
        for k in range(1, n_out):
            shared(k, x_ref, x_all.at[o], xs_send, xs_recv).wait_recv()
        row = lax.broadcasted_iota(jnp.int32, (rows, members), 0) // per_member
        own = row == lax.broadcasted_iota(jnp.int32, (rows, members), 1)
        for m in range(n_out):
            dots = lax.dot_general(
                x_all[m], a_all[m], (((1,), (1,)), ((), ())),
                preferred_element_type=F32,
            )
            dots = jnp.where(own, dots, 0.0)
            high = dots.astype(BF16)
            rest = dots - high.astype(F32)
            mid = rest.astype(BF16)
            low = (rest - mid.astype(F32)).astype(BF16)
            for d in range(2):
                cols = slice(d * nh, (d + 1) * nh)
                b_part = b_ref[m, :, cols]
                acc[m * rows : (m + 1) * rows, cols] = (
                    jnp.dot(high, b_part, preferred_element_type=F32)
                    + jnp.dot(mid, b_part, preferred_element_type=F32)
                    + jnp.dot(low, b_part, preferred_element_type=F32)
                )

    def start_update():
        for k in range(1, n_pop):
            block_to(k).wait_recv()

    todo = []
    halves = 2 if kd % 256 == 0 and pieces % 2 == 0 else 1
    ready = max(1, n_chip // 2)
    last = n_chip - 1
    for t in range(n_chip):
        if t == ready:
            todo = [start_rows, start_update] + todo
        for n, s in enumerate(order):
            for d in range(2):
                if t:
                    ring(d, t - 1, s).wait_recv()
                    if t < last:
                        ring(d, t, s).start()
                    across(d, t, s, core).start()
            if t >= ready:
                for _ in range(min(3, len(todo))):
                    todo.pop(0)()
            if t == last and n:
                before = order[n - 1]
                for d in range(2):
                    across(d, t, before, 1 - core).wait_recv()
                if before == pieces:
                    for d in range(2):
                        update(d, t)
                elif halves == 2 and before == pieces // 2 - 1:
                    for d in range(2):
                        project(d, t, 2, 0)
        if t == last:
            for d in range(2):
                across(d, t, order[-1], 1 - core).wait_recv()
                project(d, t, halves, halves - 1)
        else:
            for s in order:
                for d in range(2):
                    across(d, t, s, 1 - core).wait_recv()
            for d in range(2):
                todo.append(functools.partial(update, d, t))
                todo.append(functools.partial(project, d, t))

    for t in range(n_chip):
        for s in order:
            for d in range(2):
                if t < n_chip - 1:
                    ring(d, t, s).wait_send()
                across(d, t, s, core).wait_send()
    for k in range(1, n_out):
        shared(k, a_ref, a_all.at[o], as_send, as_recv).wait_send()
        shared(k, x_ref, x_all.at[o], xs_send, xs_recv).wait_send()
    for k in range(1, n_pop):
        block_to(k).wait_send()


def solution(mesh):
    n_pop, n_out = mesh.shape["pop"], mesh.shape["out"]
    n_chip = n_pop // CORES

    def step(inputs, projection, factor_a, factor_b, fitness_w, elite_idx):
        rows, d_in = inputs.shape
        kd, n_cols = projection.shape
        members, elite = factor_a.shape[0], elite_idx.shape[0]
        nh = n_cols // 2
        pieces = min(4, kd // 16)
        scale = math.sqrt(d_in / (n_pop * elite))
        dma = pltpu.SemaphoreType.DMA
        hbm, vmem = pl.BlockSpec(memory_space=pltpu.HBM), pl.BlockSpec(memory_space=pltpu.VMEM)
        total, update_sum = pl.pallas_call(
            functools.partial(kernel, n_pop, n_out, pieces),
            out_shape=(
                jax.ShapeDtypeStruct((n_out * rows, n_cols), F32),
                jax.ShapeDtypeStruct((kd, n_cols), F32),
            ),
            in_specs=[hbm] * 6,
            out_specs=(vmem, vmem),
            scratch_shapes=[
                pltpu.VMEM((2, n_chip, CORES * kd, nh), BF16),
                pltpu.VMEM((2, n_chip, CORES, elite, nh), BF16),
                pltpu.VMEM((n_out, rows, d_in), BF16),
                pltpu.VMEM((n_out, members, d_in), BF16),
                pltpu.VMEM((n_pop, elite, kd), BF16),
                pltpu.VMEM((n_pop, elite, kd), BF16),
                pltpu.VMEM((n_out, members, n_cols), BF16),
                pltpu.VMEM((1, n_out * members), F32),
                pltpu.VMEM((1, elite), jnp.int32),
                dma((2, n_chip, pieces + 1)),
                dma((2, n_chip, pieces + 1)),
                dma((2, n_chip, pieces + 1)),
                dma((2, n_chip, pieces + 1)),
                dma((n_out,)),
                dma((n_out,)),
                dma((n_out,)),
                dma((n_out,)),
                dma((n_pop,)),
                dma((n_pop,)),
                dma((7,)),
            ],
            compiler_params=pltpu.CompilerParams(
                collective_id=0, has_side_effects=True, vmem_limit_bytes=60 * 2**20
            ),
        )(
            inputs,
            projection,
            factor_a,
            factor_b.reshape(n_out, members, n_cols),
            fitness_w.reshape(1, -1),
            elite_idx.reshape(1, -1),
        )
        return total.astype(BF16), update_sum * scale

    return jax.shard_map(
        step,
        mesh=mesh,
        in_specs=(
            P(("pop", "out"), None),
            P("pop", "out"),
            P(("pop", "out"), None),
            P("pop", "out"),
            P("pop"),
            P("pop"),
        ),
        out_specs=(P("pop", "out"), P("pop", "out")),
        check_vma=False,
    )
```

```python
import functools
import math

import jax
import jax.numpy as jnp
from jax import lax
from jax.experimental import pallas as pl
from jax.experimental.pallas import tpu as pltpu
from jax.sharding import PartitionSpec as P

MESH = pl.DeviceIdType.MESH
F32, BF16 = jnp.float32, jnp.bfloat16
CORES, Y = 2, 2


def chip_at(pos, n_chip):
    z_len = n_chip // Y
    y = pos // z_len
    z = pos * (1 - y) + (n_chip - 1 - pos) * y
    return z * Y + y


def kernel(
    n_pop, n_out, pieces, scale,
    x_ref, w_ref, a_ref, b_hbm, f_hbm, e_hbm,
    out_ref, upd_hbm,
    acc, upd_ref, wbuf, bbuf, x_all, a_all, s_src, s_all, b_ref, f_ref, e_ref,
    ring_send, ring_recv, pair_send, pair_recv,
    xs_send, xs_recv, as_send, as_recv, s_send, s_recv, loc_sem,
):
    n_chip = n_pop // CORES
    z_len = n_chip // Y
    p, o = lax.axis_index("pop"), lax.axis_index("out")
    core, chip = p % CORES, p // CORES
    y, z = chip % Y, chip // Y
    pos = z * (1 - y) + (n_chip - 1 - z) * y
    kd, n_cols = w_ref.shape
    nh = n_cols // 2
    rows, d_in = x_ref.shape
    members = a_ref.shape[0]
    per_member = rows // members
    elite = e_ref.shape[1]
    depth = kd // pieces

    nxt = chip_at((pos + 1) % n_chip, n_chip) * CORES + core
    prv = chip_at((pos + n_chip - 1) % n_chip, n_chip) * CORES + core
    to = (nxt, prv)
    pair = chip * CORES + (1 - core)

    x_own = pltpu.make_async_copy(x_ref, x_all.at[o], loc_sem.at[0])
    a_own = pltpu.make_async_copy(a_ref, a_all.at[o], loc_sem.at[1])
    w_own = [
        pltpu.make_async_copy(
            w_ref.at[:, pl.ds(d * nh, nh)],
            wbuf.at[d, 0, pl.ds(pl.multiple_of(core * kd, kd), kd)],
            loc_sem.at[2 + d],
        )
        for d in range(2)
    ]
    small = [
        pltpu.make_async_copy(src, dst, loc_sem.at[4 + k])
        for k, (src, dst) in enumerate(((e_hbm, e_ref), (b_hbm, b_ref), (f_hbm, f_ref)))
    ]
    for own in (*small, a_own, x_own, *w_own):
        own.start()

    barrier = pltpu.get_barrier_semaphore()
    for k in range(1, n_pop):
        pl.semaphore_signal(
            barrier, inc=1, device_id={"pop": (p + k) % n_pop}, device_id_type=MESH
        )
    for k in range(1, n_out):
        pl.semaphore_signal(
            barrier, inc=1, device_id={"out": (o + k) % n_out}, device_id_type=MESH
        )
    pl.semaphore_wait(barrier, n_pop - 1 + n_out - 1)

    def piece(d, t, s, c):
        if s == pieces:
            return bbuf.at[d, t, c]
        return wbuf.at[
            d, t, pl.ds(pl.multiple_of(c * kd + s * depth, depth), depth)
        ]

    def source(d, t, s):
        if t == 0 and s < pieces:
            return w_ref.at[pl.ds(s * depth, depth), pl.ds(d * nh, nh)]
        return piece(d, t, s, core)

    def ring(d, t, s):
        return pltpu.make_async_remote_copy(
            src_ref=source(d, t, s),
            dst_ref=piece(d, t + 1, s, core),
            send_sem=ring_send.at[d, t, s],
            recv_sem=ring_recv.at[d, t, s],
            device_id={"pop": to[d]},
            device_id_type=MESH,
        )

    def across(d, t, s, c):
        return pltpu.make_async_remote_copy(
            src_ref=source(d, t, s) if c is core else piece(d, t, s, c),
            dst_ref=piece(d, t, s, c),
            send_sem=pair_send.at[d, t, s],
            recv_sem=pair_recv.at[d, t, s],
            device_id={"pop": pair},
            device_id_type=MESH,
        )

    def shared(k, src, dst, send, recv):
        return pltpu.make_async_remote_copy(
            src_ref=src,
            dst_ref=dst,
            send_sem=send.at[k],
            recv_sem=recv.at[k],
            device_id={"out": (o + k) % n_out},
            device_id_type=MESH,
        )

    def block_to(k):
        return pltpu.make_async_remote_copy(
            src_ref=s_src.at[(p + k) % n_pop],
            dst_ref=s_all.at[p],
            send_sem=s_send.at[k],
            recv_sem=s_recv.at[k],
            device_id={"pop": (p + k) % n_pop},
            device_id_type=MESH,
        )

    order = [0, pieces, *range(1, pieces)]
    for s in range(pieces):
        for d in range(2):
            ring(d, 0, s).start()
            across(d, 0, s, core).start()
        if s == 0:
            for k in range(1, n_out):
                shared(k, a_ref, a_all.at[o], as_send, as_recv).start()
            for k in range(1, n_out):
                shared(k, x_ref, x_all.at[o], xs_send, xs_recv).start()
            for own in small:
                own.wait()
            turned = lax.broadcasted_iota(jnp.int32, (elite, elite), 0)
            turned = turned == lax.broadcasted_iota(jnp.int32, (elite, elite), 1)
            ids = jnp.sum(
                jnp.where(turned, e_ref[...].astype(F32), 0.0), axis=1, keepdims=True
            ).astype(jnp.int32)

            def picks(m):
                at = lax.broadcasted_iota(jnp.int32, (elite, members), 1) + m * members
                return (at == ids).astype(F32).astype(BF16)

            for d in range(2):
                total = jnp.zeros((elite, nh), F32)
                for m in range(n_out):
                    total += jnp.dot(
                        picks(m), b_ref[m, :, d * nh : (d + 1) * nh],
                        preferred_element_type=F32,
                    )
                bbuf[d, 0, core] = total.astype(BF16)
            upd_ref[...] = jnp.zeros_like(upd_ref)
    for d in range(2):
        ring(d, 0, pieces).start()
        across(d, 0, pieces, core).start()

    a_own.wait()
    for k in range(1, n_out):
        shared(k, a_ref, a_all.at[o], as_send, as_recv).wait_recv()
    every = lax.broadcasted_iota(jnp.int32, (elite, n_out * members), 1)
    weight = jnp.sum(jnp.where(every == ids, f_ref[...], 0.0), axis=1, keepdims=True)
    for q in range(n_pop):
        block = jnp.zeros((elite, kd), F32)
        for m in range(n_out):
            block += jnp.dot(
                picks(m), a_all[m, :, q * kd : (q + 1) * kd],
                preferred_element_type=F32,
            )
        s_src[q] = (weight * block).astype(BF16)
    s_all[p] = s_src[p]
    for k in range(1, n_pop):
        block_to(k).start()

    for own in w_own:
        own.wait()

    def chip_of(d, t):
        return chip_at((pos + (n_chip - t if d == 0 else t)) % n_chip, n_chip)

    tile = min(nh, 512)

    def project(d, t, parts=1, part=0):
        off = pl.multiple_of(chip_of(d, t) * (CORES * kd), CORES * kd)
        x_part = x_all[:, :, pl.ds(off, CORES * kd)].reshape(n_out * rows, CORES * kd)
        take = kd // parts
        for j in range(nh // tile):
            lo, cols = d * nh + j * tile, slice(j * tile, (j + 1) * tile)
            if parts == 1:
                more = jnp.dot(x_part, wbuf[d, t, :, cols], preferred_element_type=F32)
            else:
                more = 0.0
                for c in range(CORES):
                    at = c * kd + part * take
                    more += jnp.dot(
                        x_part[:, at : at + take], wbuf[d, t, at : at + take, cols],
                        preferred_element_type=F32,
                    )
            acc[:, lo : lo + tile] += more

    def update(d, t):
        for c in range(CORES):
            upd_ref[:, d * nh : (d + 1) * nh] += lax.dot_general(
                s_all[chip_of(d, t) * CORES + c], bbuf[d, t, c],
                (((0,), (0,)), ((), ())), preferred_element_type=F32,
            )

    def start_rows():
        x_own.wait()
        for k in range(1, n_out):
            shared(k, x_ref, x_all.at[o], xs_send, xs_recv).wait_recv()
        row = lax.broadcasted_iota(jnp.int32, (rows, members), 0) // per_member
        own = row == lax.broadcasted_iota(jnp.int32, (rows, members), 1)
        for m in range(n_out):
            dots = lax.dot_general(
                x_all[m], a_all[m], (((1,), (1,)), ((), ())),
                preferred_element_type=F32,
            )
            dots = jnp.where(own, dots, 0.0)
            high = dots.astype(BF16)
            rest = dots - high.astype(F32)
            mid = rest.astype(BF16)
            low = (rest - mid.astype(F32)).astype(BF16)
            for d in range(2):
                cols = slice(d * nh, (d + 1) * nh)
                b_part = b_ref[m, :, cols]
                acc[m * rows : (m + 1) * rows, cols] = (
                    jnp.dot(high, b_part, preferred_element_type=F32)
                    + jnp.dot(mid, b_part, preferred_element_type=F32)
                    + jnp.dot(low, b_part, preferred_element_type=F32)
                )

    def start_update():
        for k in range(1, n_pop):
            block_to(k).wait_recv()

    todo = []
    halves = 2 if kd % 256 == 0 and pieces % 2 == 0 else 1
    ready = max(1, n_chip // 2)
    last = n_chip - 1
    upd_out = pltpu.make_async_copy(upd_ref, upd_hbm, loc_sem.at[7])
    for t in range(n_chip):
        if t == ready:
            todo = [start_rows, start_update] + todo
        for n, s in enumerate(order):
            for d in range(2):
                if t:
                    ring(d, t - 1, s).wait_recv()
                    if t < last:
                        ring(d, t, s).start()
                    across(d, t, s, core).start()
            if t >= ready:
                for _ in range(min(2, len(todo))):
                    todo.pop(0)()
            if t == last and n:
                before = order[n - 1]
                for d in range(2):
                    across(d, t, before, 1 - core).wait_recv()
                if before == pieces:
                    for d in range(2):
                        update(d, t)
                    upd_ref[...] = upd_ref[...] * scale
                    upd_out.start()
                elif halves == 2 and before == pieces // 2 - 1:
                    for d in range(2):
                        project(d, t, 2, 0)
        if t == last:
            for d in range(2):
                across(d, t, order[-1], 1 - core).wait_recv()
                project(d, t, halves, halves - 1)
                cols = slice(d * nh, (d + 1) * nh)
                out_ref[:, cols] = acc[:, cols].astype(BF16)
            upd_out.wait()
        else:
            for s in order:
                for d in range(2):
                    across(d, t, s, 1 - core).wait_recv()
            for d in range(2):
                todo.append(functools.partial(update, d, t))
                todo.append(functools.partial(project, d, t))

    for t in range(n_chip):
        for s in order:
            for d in range(2):
                if t < n_chip - 1:
                    ring(d, t, s).wait_send()
                across(d, t, s, core).wait_send()
    for k in range(1, n_out):
        shared(k, a_ref, a_all.at[o], as_send, as_recv).wait_send()
        shared(k, x_ref, x_all.at[o], xs_send, xs_recv).wait_send()
    for k in range(1, n_pop):
        block_to(k).wait_send()


def hand_on(cuts, total_ref, sum_ref, out_ref, upd_ref, total, update, in_sem, out_sem):
    arrays = ((total_ref, total, out_ref), (sum_ref, update, upd_ref))
    into, out = [], []
    for cut in range(cuts):
        for k, (src, mid, dst) in enumerate(arrays):
            size = src.shape[0] // cuts
            at = pl.ds(cut * size, size)
            into.append(pltpu.make_async_copy(src.at[at], mid.at[at], in_sem.at[k, cut]))
            out.append(pltpu.make_async_copy(mid.at[at], dst.at[at], out_sem.at[k, cut]))
    for copy in into:
        copy.start()
    for arrived, copy in zip(into, out):
        arrived.wait()
        copy.start()
    for copy in out:
        copy.wait()


def solution(mesh):
    n_pop, n_out = mesh.shape["pop"], mesh.shape["out"]
    n_chip = n_pop // CORES

    def step(inputs, projection, factor_a, factor_b, fitness_w, elite_idx):
        rows, d_in = inputs.shape
        kd, n_cols = projection.shape
        members, elite = factor_a.shape[0], elite_idx.shape[0]
        nh = n_cols // 2
        pieces = min(8, kd // 16)
        scale = math.sqrt(d_in / (n_pop * elite))
        dma = pltpu.SemaphoreType.DMA
        hbm, vmem = pl.BlockSpec(memory_space=pltpu.HBM), pl.BlockSpec(memory_space=pltpu.VMEM)
        total, update_sum = pl.pallas_call(
            functools.partial(kernel, n_pop, n_out, pieces, scale),
            out_shape=(
                jax.ShapeDtypeStruct((n_out * rows, n_cols), BF16),
                jax.ShapeDtypeStruct((kd, n_cols), F32),
            ),
            in_specs=[hbm] * 6,
            out_specs=(vmem, pl.BlockSpec(memory_space=pl.ANY)),
            scratch_shapes=[
                pltpu.VMEM((n_out * rows, n_cols), F32),
                pltpu.VMEM((kd, n_cols), F32),
                pltpu.VMEM((2, n_chip, CORES * kd, nh), BF16),
                pltpu.VMEM((2, n_chip, CORES, elite, nh), BF16),
                pltpu.VMEM((n_out, rows, d_in), BF16),
                pltpu.VMEM((n_out, members, d_in), BF16),
                pltpu.VMEM((n_pop, elite, kd), BF16),
                pltpu.VMEM((n_pop, elite, kd), BF16),
                pltpu.VMEM((n_out, members, n_cols), BF16),
                pltpu.VMEM((1, n_out * members), F32),
                pltpu.VMEM((1, elite), jnp.int32),
                dma((2, n_chip, pieces + 1)),
                dma((2, n_chip, pieces + 1)),
                dma((2, n_chip, pieces + 1)),
                dma((2, n_chip, pieces + 1)),
                dma((n_out,)),
                dma((n_out,)),
                dma((n_out,)),
                dma((n_out,)),
                dma((n_pop,)),
                dma((n_pop,)),
                dma((8,)),
            ],
            compiler_params=pltpu.CompilerParams(
                collective_id=0, has_side_effects=True, vmem_limit_bytes=60 * 2**20
            ),
        )(
            inputs,
            projection,
            factor_a,
            factor_b.reshape(n_out, members, n_cols),
            fitness_w.reshape(1, -1),
            elite_idx.reshape(1, -1),
        )
        cuts = 4
        return pl.pallas_call(
            functools.partial(hand_on, cuts),
            out_shape=(
                jax.ShapeDtypeStruct(total.shape, BF16),
                jax.ShapeDtypeStruct(update_sum.shape, F32),
            ),
            in_specs=[pl.BlockSpec(memory_space=pl.ANY)] * 2,
            out_specs=(pl.BlockSpec(memory_space=pl.ANY),) * 2,
            scratch_shapes=[
                pltpu.VMEM(total.shape, BF16),
                pltpu.VMEM(update_sum.shape, F32),
                dma((2, cuts)),
                dma((2, cuts)),
            ],
        )(total, update_sum)

    return jax.shard_map(
        step,
        mesh=mesh,
        in_specs=(
            P(("pop", "out"), None),
            P("pop", "out"),
            P(("pop", "out"), None),
            P("pop", "out"),
            P("pop"),
            P("pop"),
        ),
        out_specs=(P("pop", "out"), P("pop", "out")),
        check_vma=False,
    )
```

```python
import functools
import math

import jax
import jax.numpy as jnp
from jax import lax
from jax.experimental import pallas as pl
from jax.experimental.pallas import tpu as pltpu
from jax.sharding import PartitionSpec as P

MESH = pl.DeviceIdType.MESH
F32, BF16 = jnp.float32, jnp.bfloat16
CORES, Y = 2, 2


def chip_at(pos, n_chip):
    z_len = n_chip // Y
    y = pos // z_len
    z = pos * (1 - y) + (n_chip - 1 - pos) * y
    return z * Y + y


def kernel(
    n_pop, n_out, pieces, scale,
    x_ref, w_ref, a_ref, b_hbm, f_hbm, e_hbm,
    out_ref, upd_hbm,
    acc, upd_ref, wbuf, bbuf, x_all, a_all, s_src, s_all, b_ref, f_ref, e_ref,
    ring_send, ring_recv, pair_send, pair_recv,
    xs_send, xs_recv, as_send, as_recv, s_send, s_recv, loc_sem,
):
    n_chip = n_pop // CORES
    z_len = n_chip // Y
    p, o = lax.axis_index("pop"), lax.axis_index("out")
    core, chip = p % CORES, p // CORES
    y, z = chip % Y, chip // Y
    pos = z * (1 - y) + (n_chip - 1 - z) * y
    kd, n_cols = w_ref.shape
    nh = n_cols // 2
    rows, d_in = x_ref.shape
    members = a_ref.shape[0]
    per_member = rows // members
    elite = e_ref.shape[1]
    depth = kd // pieces

    nxt = chip_at((pos + 1) % n_chip, n_chip) * CORES + core
    prv = chip_at((pos + n_chip - 1) % n_chip, n_chip) * CORES + core
    to = (nxt, prv)
    pair = chip * CORES + (1 - core)

    x_own = pltpu.make_async_copy(x_ref, x_all.at[o], loc_sem.at[0])
    a_own = pltpu.make_async_copy(a_ref, a_all.at[o], loc_sem.at[1])
    w_own = [
        pltpu.make_async_copy(
            w_ref.at[:, pl.ds(d * nh, nh)],
            wbuf.at[d, 0, pl.ds(pl.multiple_of(core * kd, kd), kd)],
            loc_sem.at[2 + d],
        )
        for d in range(2)
    ]
    small = [
        pltpu.make_async_copy(src, dst, loc_sem.at[4 + k])
        for k, (src, dst) in enumerate(((e_hbm, e_ref), (b_hbm, b_ref), (f_hbm, f_ref)))
    ]
    for own in (*small, a_own, x_own, *w_own):
        own.start()

    barrier = pltpu.get_barrier_semaphore()
    for k in range(1, n_pop):
        pl.semaphore_signal(
            barrier, inc=1, device_id={"pop": (p + k) % n_pop}, device_id_type=MESH
        )
    for k in range(1, n_out):
        pl.semaphore_signal(
            barrier, inc=1, device_id={"out": (o + k) % n_out}, device_id_type=MESH
        )
    pl.semaphore_wait(barrier, n_pop - 1 + n_out - 1)

    def piece(d, t, s, c):
        if s == pieces:
            return bbuf.at[d, t, c]
        return wbuf.at[
            d, t, pl.ds(pl.multiple_of(c * kd + s * depth, depth), depth)
        ]

    def source(d, t, s):
        if t == 0 and s < pieces:
            return w_ref.at[pl.ds(s * depth, depth), pl.ds(d * nh, nh)]
        return piece(d, t, s, core)

    def ring(d, t, s):
        return pltpu.make_async_remote_copy(
            src_ref=source(d, t, s),
            dst_ref=piece(d, t + 1, s, core),
            send_sem=ring_send.at[d, t, s],
            recv_sem=ring_recv.at[d, t, s],
            device_id={"pop": to[d]},
            device_id_type=MESH,
        )

    def across(d, t, s, c):
        return pltpu.make_async_remote_copy(
            src_ref=source(d, t, s) if c is core else piece(d, t, s, c),
            dst_ref=piece(d, t, s, c),
            send_sem=pair_send.at[d, t, s],
            recv_sem=pair_recv.at[d, t, s],
            device_id={"pop": pair},
            device_id_type=MESH,
        )

    def shared(k, src, dst, send, recv):
        return pltpu.make_async_remote_copy(
            src_ref=src,
            dst_ref=dst,
            send_sem=send.at[k],
            recv_sem=recv.at[k],
            device_id={"out": (o + k) % n_out},
            device_id_type=MESH,
        )

    def block_to(k):
        return pltpu.make_async_remote_copy(
            src_ref=s_src.at[(p + k) % n_pop],
            dst_ref=s_all.at[p],
            send_sem=s_send.at[k],
            recv_sem=s_recv.at[k],
            device_id={"pop": (p + k) % n_pop},
            device_id_type=MESH,
        )

    order = [0, pieces, *range(1, pieces)]
    for s in range(pieces):
        for d in range(2):
            ring(d, 0, s).start()
            across(d, 0, s, core).start()
        if s == 0:
            for k in range(1, n_out):
                shared(k, a_ref, a_all.at[o], as_send, as_recv).start()
            for k in range(1, n_out):
                shared(k, x_ref, x_all.at[o], xs_send, xs_recv).start()
            for own in small:
                own.wait()
            turned = lax.broadcasted_iota(jnp.int32, (elite, elite), 0)
            turned = turned == lax.broadcasted_iota(jnp.int32, (elite, elite), 1)
            ids = jnp.sum(
                jnp.where(turned, e_ref[...].astype(F32), 0.0), axis=1, keepdims=True
            ).astype(jnp.int32)

            def picks(m):
                at = lax.broadcasted_iota(jnp.int32, (elite, members), 1) + m * members
                return (at == ids).astype(F32).astype(BF16)

            for d in range(2):
                total = jnp.zeros((elite, nh), F32)
                for m in range(n_out):
                    total += jnp.dot(
                        picks(m), b_ref[m, :, d * nh : (d + 1) * nh],
                        preferred_element_type=F32,
                    )
                bbuf[d, 0, core] = total.astype(BF16)
            upd_ref[...] = jnp.zeros_like(upd_ref)
    for d in range(2):
        ring(d, 0, pieces).start()
        across(d, 0, pieces, core).start()

    a_own.wait()
    for k in range(1, n_out):
        shared(k, a_ref, a_all.at[o], as_send, as_recv).wait_recv()
    every = lax.broadcasted_iota(jnp.int32, (elite, n_out * members), 1)
    weight = jnp.sum(jnp.where(every == ids, f_ref[...], 0.0), axis=1, keepdims=True)
    for q in range(n_pop):
        block = jnp.zeros((elite, kd), F32)
        for m in range(n_out):
            block += jnp.dot(
                picks(m), a_all[m, :, q * kd : (q + 1) * kd],
                preferred_element_type=F32,
            )
        s_src[q] = (weight * block).astype(BF16)
    s_all[p] = s_src[p]
    for k in range(1, n_pop):
        block_to(k).start()

    for own in w_own:
        own.wait()

    def chip_of(d, t):
        return chip_at((pos + (n_chip - t if d == 0 else t)) % n_chip, n_chip)

    tile = min(nh, 512)

    def project(d, t, parts=1, part=0):
        off = pl.multiple_of(chip_of(d, t) * (CORES * kd), CORES * kd)
        x_part = x_all[:, :, pl.ds(off, CORES * kd)].reshape(n_out * rows, CORES * kd)
        take = kd // parts
        for j in range(nh // tile):
            lo, cols = d * nh + j * tile, slice(j * tile, (j + 1) * tile)
            if parts == 1:
                more = jnp.dot(x_part, wbuf[d, t, :, cols], preferred_element_type=F32)
            else:
                more = 0.0
                for c in range(CORES):
                    at = c * kd + part * take
                    more += jnp.dot(
                        x_part[:, at : at + take], wbuf[d, t, at : at + take, cols],
                        preferred_element_type=F32,
                    )
            acc[:, lo : lo + tile] += more

    def update(d, t):
        for c in range(CORES):
            upd_ref[:, d * nh : (d + 1) * nh] += lax.dot_general(
                s_all[chip_of(d, t) * CORES + c], bbuf[d, t, c],
                (((0,), (0,)), ((), ())), preferred_element_type=F32,
            )

    def start_rows():
        x_own.wait()
        for k in range(1, n_out):
            shared(k, x_ref, x_all.at[o], xs_send, xs_recv).wait_recv()
        row = lax.broadcasted_iota(jnp.int32, (rows, members), 0) // per_member
        own = row == lax.broadcasted_iota(jnp.int32, (rows, members), 1)
        for m in range(n_out):
            dots = lax.dot_general(
                x_all[m], a_all[m], (((1,), (1,)), ((), ())),
                preferred_element_type=F32,
            )
            dots = jnp.where(own, dots, 0.0)
            high = dots.astype(BF16)
            rest = dots - high.astype(F32)
            mid = rest.astype(BF16)
            low = (rest - mid.astype(F32)).astype(BF16)
            for d in range(2):
                cols = slice(d * nh, (d + 1) * nh)
                b_part = b_ref[m, :, cols]
                acc[m * rows : (m + 1) * rows, cols] = (
                    jnp.dot(high, b_part, preferred_element_type=F32)
                    + jnp.dot(mid, b_part, preferred_element_type=F32)
                    + jnp.dot(low, b_part, preferred_element_type=F32)
                )

    def start_update():
        for k in range(1, n_pop):
            block_to(k).wait_recv()

    todo = []
    halves = 2 if kd % 256 == 0 and pieces % 2 == 0 else 1
    ready = max(1, n_chip // 2)
    last = n_chip - 1
    upd_out = pltpu.make_async_copy(upd_ref, upd_hbm, loc_sem.at[7])
    for t in range(n_chip):
        if t == ready:
            todo = [start_rows, start_update] + todo
        for n, s in enumerate(order):
            for d in range(2):
                if t:
                    ring(d, t - 1, s).wait_recv()
                    if t < last:
                        ring(d, t, s).start()
                    across(d, t, s, core).start()
            if t >= ready:
                for _ in range(min(3, len(todo))):
                    todo.pop(0)()
            if t == last and n:
                before = order[n - 1]
                for d in range(2):
                    across(d, t, before, 1 - core).wait_recv()
                if before == pieces:
                    for d in range(2):
                        update(d, t)
                    upd_ref[...] = upd_ref[...] * scale
                    upd_out.start()
                elif halves == 2 and before == pieces // 2 - 1:
                    for d in range(2):
                        project(d, t, 2, 0)
        if t == last:
            for d in range(2):
                across(d, t, order[-1], 1 - core).wait_recv()
                project(d, t, halves, halves - 1)
                cols = slice(d * nh, (d + 1) * nh)
                out_ref[:, cols] = acc[:, cols].astype(BF16)
            upd_out.wait()
        else:
            for s in order:
                for d in range(2):
                    across(d, t, s, 1 - core).wait_recv()
            for d in range(2):
                todo.append(functools.partial(update, d, t))
                todo.append(functools.partial(project, d, t))

    for t in range(n_chip):
        for s in order:
            for d in range(2):
                if t < n_chip - 1:
                    ring(d, t, s).wait_send()
                across(d, t, s, core).wait_send()
    for k in range(1, n_out):
        shared(k, a_ref, a_all.at[o], as_send, as_recv).wait_send()
        shared(k, x_ref, x_all.at[o], xs_send, xs_recv).wait_send()
    for k in range(1, n_pop):
        block_to(k).wait_send()


def hand_on(cuts, total_ref, sum_ref, out_ref, upd_ref, total, update, in_sem, out_sem):
    arrays = ((total_ref, total, out_ref), (sum_ref, update, upd_ref))
    into, out = [], []
    for cut in range(cuts):
        for k, (src, mid, dst) in enumerate(arrays):
            size = src.shape[0] // cuts
            at = pl.ds(cut * size, size)
            into.append(pltpu.make_async_copy(src.at[at], mid.at[at], in_sem.at[k, cut]))
            out.append(pltpu.make_async_copy(mid.at[at], dst.at[at], out_sem.at[k, cut]))
    for copy in into:
        copy.start()
    for arrived, copy in zip(into, out):
        arrived.wait()
        copy.start()
    for copy in out:
        copy.wait()


def solution(mesh):
    n_pop, n_out = mesh.shape["pop"], mesh.shape["out"]
    n_chip = n_pop // CORES

    def step(inputs, projection, factor_a, factor_b, fitness_w, elite_idx):
        rows, d_in = inputs.shape
        kd, n_cols = projection.shape
        members, elite = factor_a.shape[0], elite_idx.shape[0]
        nh = n_cols // 2
        pieces = min(4, kd // 16)
        scale = math.sqrt(d_in / (n_pop * elite))
        dma = pltpu.SemaphoreType.DMA
        hbm, vmem = pl.BlockSpec(memory_space=pltpu.HBM), pl.BlockSpec(memory_space=pltpu.VMEM)
        total, update_sum = pl.pallas_call(
            functools.partial(kernel, n_pop, n_out, pieces, scale),
            out_shape=(
                jax.ShapeDtypeStruct((n_out * rows, n_cols), BF16),
                jax.ShapeDtypeStruct((kd, n_cols), F32),
            ),
            in_specs=[hbm] * 6,
            out_specs=(vmem, pl.BlockSpec(memory_space=pl.ANY)),
            scratch_shapes=[
                pltpu.VMEM((n_out * rows, n_cols), F32),
                pltpu.VMEM((kd, n_cols), F32),
                pltpu.VMEM((2, n_chip, CORES * kd, nh), BF16),
                pltpu.VMEM((2, n_chip, CORES, elite, nh), BF16),
                pltpu.VMEM((n_out, rows, d_in), BF16),
                pltpu.VMEM((n_out, members, d_in), BF16),
                pltpu.VMEM((n_pop, elite, kd), BF16),
                pltpu.VMEM((n_pop, elite, kd), BF16),
                pltpu.VMEM((n_out, members, n_cols), BF16),
                pltpu.VMEM((1, n_out * members), F32),
                pltpu.VMEM((1, elite), jnp.int32),
                dma((2, n_chip, pieces + 1)),
                dma((2, n_chip, pieces + 1)),
                dma((2, n_chip, pieces + 1)),
                dma((2, n_chip, pieces + 1)),
                dma((n_out,)),
                dma((n_out,)),
                dma((n_out,)),
                dma((n_out,)),
                dma((n_pop,)),
                dma((n_pop,)),
                dma((8,)),
            ],
            compiler_params=pltpu.CompilerParams(
                collective_id=0, has_side_effects=True, vmem_limit_bytes=60 * 2**20
            ),
        )(
            inputs,
            projection,
            factor_a,
            factor_b.reshape(n_out, members, n_cols),
            fitness_w.reshape(1, -1),
            elite_idx.reshape(1, -1),
        )
        cuts = 4
        return pl.pallas_call(
            functools.partial(hand_on, cuts),
            out_shape=(
                jax.ShapeDtypeStruct(total.shape, BF16),
                jax.ShapeDtypeStruct(update_sum.shape, F32),
            ),
            in_specs=[pl.BlockSpec(memory_space=pl.ANY)] * 2,
            out_specs=(pl.BlockSpec(memory_space=pl.ANY),) * 2,
            scratch_shapes=[
                pltpu.VMEM(total.shape, BF16),
                pltpu.VMEM(update_sum.shape, F32),
                dma((2, cuts)),
                dma((2, cuts)),
            ],
        )(total, update_sum)

    return jax.shard_map(
        step,
        mesh=mesh,
        in_specs=(
            P(("pop", "out"), None),
            P("pop", "out"),
            P(("pop", "out"), None),
            P("pop", "out"),
            P("pop"),
            P("pop"),
        ),
        out_specs=(P("pop", "out"), P("pop", "out")),
        check_vma=False,
    )
```
